32 devices in a mesh: lat: 4 (over z), lon: 4 (over y, x), rad: 2 (over core).
Axes of the slice: x: 2, y: 2, z: 4, core: 2. Of those that a mesh axis runs over, the one named last changes fastest.
Arguments:
- velocity: float32 [3, 32, 32, 1024], P(None, 'rad', 'lat', 'lon'), may hold values from -6 to 6
- forcing: float32 [3, 32, 32, 1024], P(None, 'rad', 'lat', 'lon'), may hold values from -6 to 6
- viscosity: float32 [32, 32, 1024], P('rad', 'lat', 'lon'), may hold values from 0.1 to 10
- plate_ids: int32 [4, 128], P('lat', 'lon'), may hold values from 0 to 11, as said below
Outputs:
- new_velocity: float32 [3, 32, 32, 1024], P(None, 'rad', 'lat', 'lon')
- coarse_residual: float32 [3, 16, 16, 512], P(None, None, 'lat', 'lon')
- plate_velocity: float32 [3, 32, 1024], P(None, 'lat', 'lon')
The draws below stay inside these ranges and needn't reach their ends.
Inputs may be any that keep to these rules, and one draw needn't show every extreme that they name: `plate_ids`: every plate number from 0 to 11 names at least one face block.
All inputs are finite; a program needn't handle non-finite values.
Results may differ from the reference program's by a relative error of at most 0.0003.
Values sent between devices are 32-bit elements; how exact they have to be, the bound alone decides.
A program may use at most 64 MiB of HBM per device.

```python
import math
import jax
import jax.numpy as jnp
from jax import lax

SWEEPS = 3
PLATES = 12
FACE = 8
NR = 32
NA = 32
NO = 1024


def draw_plate_ids(key, part):
    block_rows = NA // FACE
    block_cols = NO // FACE
    plates = jax.random.randint(key, (block_rows * block_cols,), 0, PLATES, dtype=jnp.int32)
    places = jax.random.permutation(jax.random.fold_in(key, 17), block_rows * block_cols)[:PLATES]
    plates = plates.at[places].set(jnp.arange(PLATES, dtype=jnp.int32))
    return plates.reshape(block_rows, block_cols)


def levels(stream_key, extent, shards, least, high):
    factor_of, own = 1.0, jax.random.fold_in(stream_key, 6)
    for dim, shards_of in shards:
        heights = jnp.exp(jax.random.uniform(jax.random.fold_in(own, dim), (shards_of,), jnp.float32, least / len(shards), high / len(shards)))
        factor_of = factor_of * jnp.repeat(heights, extent[dim] // shards_of).reshape([-1 if axis == dim else 1 for axis in range(len(extent))])
    return factor_of


def bell_draw(key, shape, scale, reach, pieces=(), held_as=jnp.bfloat16):
    gain = levels(key, shape, pieces, -0.22, 0.18) if pieces else 1.0
    values = jax.random.normal(key, shape, jnp.float32) * scale * gain
    return jnp.minimum(jnp.maximum(values, -reach), reach).astype(held_as)


def setup_inputs(seed: int = 0) -> dict:
    arg_keys = jax.random.split(jax.random.key(seed), 5)
    velocity = bell_draw(arg_keys[0], (3, NR, NA, NO), 1.0, 6.0, ((1, 2), (2, 4), (3, 4)), jnp.float32)
    forcing = bell_draw(arg_keys[1], (3, NR, NA, NO), 1.0, 6.0, ((1, 2), (2, 4), (3, 4)), jnp.float32)
    viscosity = jnp.clip(jnp.exp(math.log(10.0) - 4.6051702 * jax.random.uniform(arg_keys[2], (NR, NA, NO), jnp.float32) ** levels(arg_keys[2], (NR, NA, NO), ((0, 2), (1, 4), (2, 4)), -0.2, 0.2)), 0.1, 10.0)
    plate_ids = draw_plate_ids(jax.random.fold_in(arg_keys[4], 71), 0)
    return dict(velocity=velocity, forcing=forcing, viscosity=viscosity, plate_ids=plate_ids)


relaxation = 0.8
neighbours = ((0, 1, 1), (2, 1, 1), (1, 0, 1), (1, 2, 1), (1, 1, 0), (1, 1, 2))

def harmonic(own_visc, other_visc):
    total = own_visc + other_visc
    positive = total > 0
    safe_total = jnp.where(positive, total, 1.0)
    return jnp.where(positive, 2.0 * own_visc * other_visc / safe_total, 0.0)

def operate(padded_vel, padded_visc):
    center_vel = padded_vel[:, 1:-1, 1:-1, 1:-1]
    own_visc = padded_visc[1:-1, 1:-1, 1:-1]
    count_rad, count_lat, count_lon = own_visc.shape
    action = 0.5 * own_visc * center_vel
    diagonal = 0.5 * own_visc
    for step_rad, step_lat, step_lon in neighbours:
        other_visc = padded_visc[step_rad:step_rad + count_rad, step_lat:step_lat + count_lat, step_lon:step_lon + count_lon]
        other_vel = padded_vel[:, step_rad:step_rad + count_rad, step_lat:step_lat + count_lat, step_lon:step_lon + count_lon]
        link_weight = harmonic(own_visc, other_visc)
        diagonal = diagonal + link_weight
        action = action + link_weight * (center_vel - other_vel)
    return (action, diagonal, center_vel, own_visc)

def relax_step(padded_vel, forcing_in, padded_visc):
    action, diagonal, center_vel, own_visc = operate(padded_vel, padded_visc)
    inside = own_visc > 0
    safe_diag = jnp.where(inside, diagonal, 1.0)
    updated = center_vel + relaxation * (forcing_in - action) / safe_diag
    return jnp.where(inside, updated, center_vel)

def restrict(residual_field):
    shape_all = residual_field.shape
    blocks = residual_field.reshape(shape_all[0], shape_all[1] // 2, 2, shape_all[2] // 2, 2, shape_all[3] // 2, 2)
    return lax.optimization_barrier(jnp.mean(blocks, axis=(2, 4, 6)))

def surface(velocity, viscosity, lat_cells, lon_cells, lat_total, lon_total):
    latitude = jnp.pi * ((lat_cells + 0.5) / lat_total - 0.5)
    longitude = 2.0 * jnp.pi * (lon_cells + 0.5) / lon_total
    lon_ones = jnp.ones_like(longitude)[None, :]
    cos_lat = jnp.cos(latitude)[:, None] * lon_ones
    radius_x = cos_lat * jnp.cos(longitude)[None, :]
    radius_y = cos_lat * jnp.sin(longitude)[None, :]
    radius_z = jnp.sin(latitude)[:, None] * lon_ones
    traction = viscosity[-1][None] * (velocity[:, -1] - velocity[:, -2])
    torque = jnp.stack([(radius_y * traction[2] - radius_z * traction[1]) * cos_lat, (radius_z * traction[0] - radius_x * traction[2]) * cos_lat, (radius_x * traction[1] - radius_y * traction[0]) * cos_lat, cos_lat])
    return (torque, (radius_x, radius_y, radius_z))

def plate_table(plate_ids):
    cell_plates = jnp.repeat(jnp.repeat(plate_ids, FACE, axis=0), FACE, axis=1)
    numbers = jnp.arange(PLATES, dtype=jnp.int32)[:, None, None]
    onehot = (cell_plates[None] == numbers).astype(jnp.float32)
    return onehot.reshape(PLATES, -1)

def rotate(rotation, onehot, radius):
    per_cell = jnp.dot(rotation, onehot, precision=lax.Precision.HIGHEST).reshape((3,) + radius[0].shape)
    radius_x, radius_y, radius_z = radius
    return jnp.stack([per_cell[1] * radius_z - per_cell[2] * radius_y, per_cell[2] * radius_x - per_cell[0] * radius_z, per_cell[0] * radius_y - per_cell[1] * radius_x])

def pad_cells(block):
    block = jnp.concatenate([block[..., -1:], block, block[..., :1]], axis=-1)
    widths = [(0, 0)] * (block.ndim - 3) + [(1, 1), (1, 1), (0, 0)]
    return jnp.pad(block, widths)

def reference(velocity, forcing, viscosity, plate_ids):
    padded_visc = pad_cells(viscosity)
    current = velocity
    for sweep_index in range(SWEEPS):
        current = relax_step(pad_cells(current), forcing, padded_visc)
    action = operate(pad_cells(current), padded_visc)[0]
    coarse_residual = restrict(forcing - action)
    torque, radius = surface(current, viscosity, jnp.arange(NA, dtype=jnp.float32), jnp.arange(NO, dtype=jnp.float32), NA, NO)
    onehot = plate_table(plate_ids)
    sums = jnp.dot(torque.reshape(4, -1), onehot.T, precision=lax.Precision.HIGHEST)
    rotation = sums[:3] / jnp.sqrt(sums[3])[None]
    return (current, coarse_residual, rotate(rotation, onehot, radius))
```

```python
import functools
import math

import jax
import jax.numpy as jnp
from jax import lax
from jax.experimental import pallas as pl
from jax.experimental.pallas import tpu as pltpu
from jax.sharding import PartitionSpec as P

SWEEPS = 3
PLATES = 12
FACE = 8
RELAX = 0.8
COMPS = 3
LANES = 128
SLOT = 32
MESH = pl.DeviceIdType.MESH
HIGHEST = lax.Precision.HIGHEST
UNROLL = 4


def harmonic(own, other):
    return 2.0 * own * other / (own + other)


def kernel(
    sizes, vel, forc, visc, ids,
    newv, coarse, plate,
    v, f, eta, w_lat, w_lon, w_rad, gain, diag,
    face_out, face_in, col_out, col_in, pairs,
    lat_sums, lon_sums, stage_out,
    load_sem, send_sem, recv_sem, s1_send, s1_recv, s2_send, s2_recv, g_send, g_recv, out_sem,
):
    n_lat, n_lon, n_rad = sizes
    n_r, n_a, n_o = visc.shape
    me_lat, me_lon, me_rad = (lax.axis_index(a) for a in ("lat", "lon", "rad"))
    lat_lo, lat_hi = me_lat > 0, me_lat < n_lat - 1
    rad_lo, rad_hi = me_rad > 0, me_rad < n_rad - 1
    lon_up, lon_dn = lax.rem(me_lon + 1, n_lon), lax.rem(me_lon + n_lon - 1, n_lon)
    is_top = me_rad == n_rad - 1

    loads = [
        pltpu.make_async_copy(visc, eta.at[pl.ds(1, n_r)], load_sem.at[0]),
        pltpu.make_async_copy(vel, v.at[0, :, pl.ds(1, n_r)], load_sem.at[1]),
        pltpu.make_async_copy(forc, f, load_sem.at[2]),
    ]
    for load in loads:
        load.start()

    barrier = pltpu.get_barrier_semaphore()

    def greet(device):
        pl.semaphore_signal(barrier, inc=1, device_id=device, device_id_type=MESH)

    expected = 2
    greet({"lon": lon_up})
    greet({"lon": lon_dn})
    for has, device in (
        (lat_lo, {"lat": me_lat - 1}), (lat_hi, {"lat": me_lat + 1}),
        (rad_lo, {"rad": me_rad - 1}), (rad_hi, {"rad": me_rad + 1}),
    ):
        pl.when(has)(functools.partial(greet, device))
        expected = expected + jnp.where(has, 1, 0)
    if n_lat - 1 > SWEEPS + 1:
        for step in range(1, n_lat):
            greet({"lat": lax.rem(me_lat + step, n_lat)})
        expected = expected + (n_lat - 1)
    if n_lon // 2 + n_rad - 1 > SWEEPS + 1:
        for step in range(1, n_lon * n_rad):
            greet({
                "lon": lax.rem(me_lon + step // n_rad, n_lon),
                "rad": lax.rem(me_rad + step % n_rad, n_rad),
            })
        expected = expected + (n_lon * n_rad - 1)

    lane_wide = lax.broadcasted_iota(jnp.int32, (n_a, n_o), 1)
    lane = lax.broadcasted_iota(jnp.int32, (n_a, LANES), 1)
    row = lax.broadcasted_iota(jnp.int32, (n_a, n_o), 0)
    reps = n_o // LANES

    zero_plane = jnp.zeros((n_a, n_o), jnp.float32)
    for has, slot in ((rad_lo, 0), (rad_hi, n_r + 1)):
        @pl.when(jnp.logical_not(has))
        def _():
            eta[slot] = zero_plane
            for t in range(SWEEPS + 1):
                for c in range(COMPS):
                    v[t, c, slot] = zero_plane
    for has, side in ((lat_lo, 0), (lat_hi, 1)):
        @pl.when(jnp.logical_not(has))
        def _():
            for t in range(SWEEPS + 1):
                face_in[t, side] = jnp.zeros(face_in.shape[2:], jnp.float32)

    def links(t):
        rows = pl.ds(0, ((COMPS + 1) if t == 0 else COMPS) * n_r)

        def remote(src, dst, k, device):
            return pltpu.make_async_remote_copy(
                src, dst, send_sem.at[t, k], recv_sem.at[t, k], device_id=device, device_id_type=MESH
            )

        out = [
            (remote(face_out.at[t, 1, rows], face_in.at[t, 0, rows], 0, {"lat": me_lat + 1}), lat_hi, lat_lo),
            (remote(face_out.at[t, 0, rows], face_in.at[t, 1, rows], 1, {"lat": me_lat - 1}), lat_lo, lat_hi),
            (remote(col_out.at[t, 1], col_in.at[t, 0], 2, {"lon": lon_up}), None, None),
            (remote(col_out.at[t, 0], col_in.at[t, 1], 3, {"lon": lon_dn}), None, None),
            (remote(v.at[t, :, n_r], v.at[t, :, 0], 4, {"rad": me_rad + 1}), rad_hi, rad_lo),
            (remote(v.at[t, :, 1], v.at[t, :, n_r + 1], 5, {"rad": me_rad - 1}), rad_lo, rad_hi),
        ]
        if t == 0:
            out += [
                (remote(eta.at[n_r], eta.at[0], 6, {"rad": me_rad + 1}), rad_hi, rad_lo),
                (remote(eta.at[1], eta.at[n_r + 1], 7, {"rad": me_rad - 1}), rad_lo, rad_hi),
            ]
        return out

    def guarded(cond, call):
        if cond is None:
            call()
        else:
            pl.when(cond)(call)

    def start(t):
        for copy, sends, _ in links(t):
            guarded(sends, copy.start)

    def arrive(t):
        for copy, _, receives in links(t):
            guarded(receives, copy.wait_recv)

    def sent(t):
        for copy, sends, _ in links(t):
            guarded(sends, copy.wait_send)

    def pack(t, k, tile, cols):
        face_out[t, 0, k] = tile[:1]
        face_out[t, 1, k] = tile[n_a - 1 :]
        low, high = cols
        hit = lane == k
        low = jnp.where(hit, pltpu.roll(tile[:, :LANES], k, 1), low)
        high = jnp.where(hit, pltpu.roll(tile[:, n_o - LANES :], lax.rem(k + 1, LANES), 1), high)
        return low, high

    def over_radius(body, init):
        def block(i, carry):
            for j in range(UNROLL):
                carry = body(i * UNROLL + j, carry)
            return carry

        return lax.fori_loop(0, n_r // UNROLL, block, init)

    no_cols = (jnp.zeros((n_a, LANES), jnp.float32),) * 2

    def shifted(t, k, tile, cols):
        col_lo, col_hi = cols
        below = jnp.where(row == 0, face_in[t, 0, k], pltpu.roll(tile, 1, 0))
        above = jnp.where(row == n_a - 1, face_in[t, 1, k], pltpu.roll(tile, n_a - 1, 0))
        from_lo = pltpu.roll(col_lo, lax.rem(LANES - k, LANES), 1)
        from_hi = pltpu.roll(col_hi, LANES - 1 - k, 1)
        west = jnp.where(lane_wide == 0, jnp.concatenate([from_lo] * reps, 1), pltpu.roll(tile, 1, 1))
        east = jnp.where(
            lane_wide == n_o - 1, jnp.concatenate([from_hi] * reps, 1), pltpu.roll(tile, n_o - 1, 1)
        )
        return below, above, west, east

    loads[0].wait()
    loads[1].wait()

    def pack_first(r, cols):
        for c in range(COMPS):
            cols = pack(0, c * n_r + r, v[0, c, r + 1], cols)
        return pack(0, COMPS * n_r + r, eta[r + 1], cols)

    low, high = over_radius(pack_first, no_cols)
    col_out[0, 0] = low
    col_out[0, 1] = high
    pl.semaphore_wait(barrier, expected)
    start(0)

    lat_cell = (me_lat * n_a + row).astype(jnp.float32)
    lon_cell = (me_lon * n_o + lane_wide).astype(jnp.float32)
    phi = math.pi * ((lat_cell + 0.5) / (n_lat * n_a) - 0.5)
    lam = (2.0 * math.pi) * (lon_cell[:1] + 0.5) / (n_lon * n_o)
    cos_lat = jnp.cos(phi)
    rx = cos_lat * jnp.cos(lam)
    ry = cos_lat * jnp.sin(lam)
    rz = jnp.sin(phi)
    blocks = ids.shape[1]
    spread_rows = lax.broadcasted_iota(jnp.int32, (blocks, n_o), 0)
    spread_cols = lax.broadcasted_iota(jnp.int32, (blocks, n_o), 1)
    spread = (spread_cols // FACE == spread_rows).astype(jnp.float32)
    numbers = lax.broadcasted_iota(jnp.int32, (SLOT, n_o), 0)
    onehots = []
    for band in range(n_a // FACE):
        own = jnp.broadcast_to(ids[band : band + 1].astype(jnp.float32), (8, blocks))
        cells = jnp.dot(own, spread, precision=HIGHEST)[:1]
        onehots.append((jnp.abs(cells - numbers.astype(jnp.float32)) < 0.5).astype(jnp.float32))

    arrive(0)

    cols_first = (col_in[0, 0], col_in[0, 1])
    w_rad[0] = harmonic(eta[1], eta[0])

    def weigh(r, carry):
        own = eta[r + 1]
        near = shifted(0, COMPS * n_r + r, own, cols_first)
        below, above, west, east = (harmonic(own, other) for other in near)
        up = harmonic(own, eta[r + 2])
        w_lat[0, r] = below
        w_lat[1, r] = above
        w_lon[0, r] = west
        w_lon[1, r] = east
        w_rad[r + 1] = up
        d = 0.5 * own + (below + above) + (west + east) + (up + w_rad[r])
        diag[r] = d
        gain[r] = RELAX / d
        return carry

    over_radius(weigh, 0)
    loads[2].wait()

    def flux(t, c, r, cols):
        tile = v[t, c, r + 1]
        below, above, west, east = shifted(t, c * n_r + r, tile, cols)
        total = (
            (w_lat[0, r] * below + w_lat[1, r] * above)
            + (w_lon[0, r] * west + w_lon[1, r] * east)
            + (w_rad[r] * v[t, c, r] + w_rad[r + 1] * v[t, c, r + 2])
        )
        return tile, f[c, r] + total

    for t in range(SWEEPS):
        if t > 0:
            arrive(t)
        cols_in = (col_in[t, 0], col_in[t, 1])

        def sweep(r, cols):
            for c in range(COMPS):
                tile, total = flux(t, c, r, cols_in)
                fresh = (1.0 - RELAX) * tile + gain[r] * total
                v[t + 1, c, r + 1] = fresh
                cols = pack(t + 1, c * n_r + r, fresh, cols)
            return cols

        low, high = over_radius(sweep, no_cols)
        col_out[t + 1, 0] = low
        col_out[t + 1, 1] = high
        start(t + 1)

    final = v.at[SWEEPS]
    store_v = pltpu.make_async_copy(final.at[:, pl.ds(1, n_r)], newv, out_sem.at[0])
    store_v.start()

    def s1_copy(step):
        return pltpu.make_async_remote_copy(
            stage_out.at[0], lat_sums.at[me_lat], s1_send.at[step - 1], s1_recv.at[me_lat],
            device_id={"lat": lax.rem(me_lat + step, n_lat)}, device_id_type=MESH,
        )

    def s2_copy(step):
        return pltpu.make_async_remote_copy(
            stage_out.at[1], lon_sums.at[me_lon], s2_send.at[step - 1], s2_recv.at[me_lon],
            device_id={
                "lon": lax.rem(me_lon + step // n_rad, n_lon),
                "rad": lax.rem(me_rad + step % n_rad, n_rad),
            },
            device_id_type=MESH,
        )

    def received(buffer, sem, index):
        pltpu.make_async_remote_copy(
            stage_out.at[0], buffer.at[index], s1_send.at[0], sem.at[index],
            device_id={"lon": lon_up}, device_id_type=MESH,
        ).wait_recv()

    @pl.when(is_top)
    def _():
        drag = [eta[n_r] * (final[c, n_r] - final[c, n_r - 1]) for c in range(COMPS)]
        twist = (
            (ry * drag[2] - rz * drag[1]) * cos_lat,
            (rz * drag[0] - rx * drag[2]) * cos_lat,
            (rx * drag[1] - ry * drag[0]) * cos_lat,
            cos_lat,
        )
        packed = jnp.zeros((1, LANES), jnp.float32)
        for band in range(n_a // FACE):
            cut = slice(band * FACE, (band + 1) * FACE)
            rows = jnp.concatenate(
                [jnp.sum(x[cut], axis=0, keepdims=True) for x in twist]
                + [jnp.zeros((4, n_o), jnp.float32)], 0,
            )
            sums = lax.dot_general(
                rows, onehots[band], (((1,), (1,)), ((), ())), precision=HIGHEST,
                preferred_element_type=jnp.float32,
            )
            packed = packed + jnp.concatenate([sums[i : i + 1] for i in range(COMPS + 1)], 1)
        stage_out[0] = packed
        lat_sums[me_lat] = packed
        for step in range(1, n_lat):
            s1_copy(step).start()
        for step in range(1, n_lat):
            received(lat_sums, s1_recv, lax.rem(me_lat + step, n_lat))
        total = lat_sums[0]
        for i in range(1, n_lat):
            total = total + lat_sums[i]
        stage_out[1] = total
        lon_sums[me_lon] = total
        for step in range(1, n_lon * n_rad):
            s2_copy(step).start()

    arrive(SWEEPS)
    cols_in = (col_in[SWEEPS, 0], col_in[SWEEPS, 1])

    def remain(q, carry):
        for c in range(COMPS):
            two = jnp.zeros((n_a, n_o), jnp.float32)
            for s in range(2):
                r = 2 * q + s
                tile, total = flux(SWEEPS, c, r, cols_in)
                two = two + (total - diag[r] * tile)
            at = pl.ds(pl.multiple_of((c * (n_r // 2) + q) * n_a, n_a), n_a)
            for h in range(reps):
                pairs[h, at] = two[:, h * LANES : (h + 1) * LANES]
        return carry

    def remain_block(i, carry):
        for j in range(2):
            carry = remain(2 * i + j, carry)
        return carry

    lax.fori_loop(0, n_r // 4, remain_block, 0)
    half = n_o // 2
    thin_r = lax.broadcasted_iota(jnp.int32, (LANES, half), 0)
    thin_c = lax.broadcasted_iota(jnp.int32, (LANES, half), 1)
    count = COMPS * (n_r // 2) * n_a // 2
    merged = jnp.zeros((count, half), jnp.float32)
    for h in range(reps):
        pick = jnp.where((thin_r + h * LANES) // 2 == thin_c, 0.125, 0.0).astype(jnp.bfloat16)
        both = pairs[h, pl.ds(0, count, stride=2)] + pairs[h, pl.ds(1, count, stride=2)]
        big = both.astype(jnp.bfloat16)
        small = (both - big.astype(jnp.float32)).astype(jnp.bfloat16)
        merged = merged + (
            jnp.dot(big, pick, preferred_element_type=jnp.float32)
            + jnp.dot(small, pick, preferred_element_type=jnp.float32)
        )
    mine = count // COMPS
    spot = pl.ds(pl.multiple_of(me_rad * mine, mine), mine)
    for c in range(COMPS):
        coarse[c, spot] = merged[c * mine : (c + 1) * mine]

    def g_copy(step):
        return pltpu.make_async_remote_copy(
            coarse.at[:, spot], coarse.at[:, spot], g_send.at[step - 1], g_recv.at[me_rad],
            device_id={"rad": lax.rem(me_rad + step, n_rad)}, device_id_type=MESH,
        )

    for step in range(1, n_rad):
        g_copy(step).start()

    for i in range(n_lon):
        @pl.when(jnp.logical_or(jnp.logical_not(is_top), me_lon != i))
        def _():
            received(lon_sums, s2_recv, i)
    total = lon_sums[0]
    for i in range(1, n_lon):
        total = total + lon_sums[i]
    area = total[:, COMPS * SLOT : (COMPS + 1) * SLOT]
    valid = lax.broadcasted_iota(jnp.int32, (1, SLOT), 1) < PLATES
    root = jnp.sqrt(jnp.where(valid, area, 1.0))
    turns = jnp.concatenate(
        [total[:, i * SLOT : (i + 1) * SLOT] / root for i in range(COMPS)]
        + [jnp.zeros((8 - COMPS, SLOT), jnp.float32)], 0,
    )
    for band in range(n_a // FACE):
        cut = slice(band * FACE, (band + 1) * FACE)
        cell = jnp.dot(turns, onehots[band], precision=HIGHEST, preferred_element_type=jnp.float32)
        ox, oy, oz = (cell[i : i + 1] for i in range(COMPS))
        plate[0, cut] = oy * rz[cut] - oz * ry[cut]
        plate[1, cut] = oz * rx[cut] - ox * rz[cut]
        plate[2, cut] = ox * ry[cut] - oy * rx[cut]

    for t in range(SWEEPS + 1):
        sent(t)

    @pl.when(is_top)
    def _():
        for step in range(1, n_lat):
            s1_copy(step).wait_send()
        for step in range(1, n_lon * n_rad):
            s2_copy(step).wait_send()

    for step in range(1, n_rad):
        source = lax.rem(me_rad + step, n_rad)
        region = coarse.at[:, pl.ds(pl.multiple_of(source * mine, mine), mine)]
        pltpu.make_async_remote_copy(
            region, region, g_send.at[0], g_recv.at[source],
            device_id={"rad": source}, device_id_type=MESH,
        ).wait_recv()
        g_copy(step).wait_send()
    store_v.wait()


def on_device(sizes, velocity, forcing, viscosity, plate_ids):
    n_lat, n_lon, n_rad = sizes
    _, n_r, n_a, n_o = velocity.shape
    rounds = SWEEPS + 1
    f32 = jnp.float32
    dma = pltpu.SemaphoreType.DMA
    in_any = pl.BlockSpec(memory_space=pl.ANY)
    in_vmem = pl.BlockSpec(memory_space=pltpu.VMEM)
    coarse_rows = n_rad * (n_r // 2) * (n_a // 2)
    new_v, coarse, plate = pl.pallas_call(
        functools.partial(kernel, sizes),
        out_shape=(
            jax.ShapeDtypeStruct(velocity.shape, f32),
            jax.ShapeDtypeStruct((COMPS, coarse_rows, n_o // 2), f32),
            jax.ShapeDtypeStruct((COMPS, n_a, n_o), f32),
        ),
        in_specs=[in_any, in_any, in_any, in_vmem],
        out_specs=(in_any, in_vmem, in_vmem),
        scratch_shapes=[
            pltpu.VMEM((rounds, COMPS, n_r + 2, n_a, n_o), f32),
            pltpu.VMEM((COMPS, n_r, n_a, n_o), f32),
            pltpu.VMEM((n_r + 2, n_a, n_o), f32),
            pltpu.VMEM((2, n_r, n_a, n_o), f32),
            pltpu.VMEM((2, n_r, n_a, n_o), f32),
            pltpu.VMEM((n_r + 1, n_a, n_o), f32),
            pltpu.VMEM((n_r, n_a, n_o), f32),
            pltpu.VMEM((n_r, n_a, n_o), f32),
            pltpu.VMEM((rounds, 2, (COMPS + 1) * n_r, 1, n_o), f32),
            pltpu.VMEM((rounds, 2, (COMPS + 1) * n_r, 1, n_o), f32),
            pltpu.VMEM((rounds, 2, n_a, LANES), f32),
            pltpu.VMEM((rounds, 2, n_a, LANES), f32),
            pltpu.VMEM((n_o // LANES, COMPS * (n_r // 2) * n_a, LANES), f32),
            pltpu.VMEM((n_lat, 1, LANES), f32),
            pltpu.VMEM((n_lon, 1, LANES), f32),
            pltpu.VMEM((2, 1, LANES), f32),
            dma((3,)),
            dma((rounds, 8)),
            dma((rounds, 8)),
            dma((n_lat,)),
            dma((n_lat,)),
            dma((n_lon * n_rad,)),
            dma((n_lon,)),
            dma((n_rad,)),
            dma((n_rad,)),
            dma((1,)),
        ],
        compiler_params=pltpu.CompilerParams(collective_id=0, has_side_effects=True),
    )(velocity, forcing, viscosity, plate_ids)
    coarse = coarse.reshape(COMPS, n_rad * (n_r // 2), n_a // 2, n_o // 2)
    return new_v, coarse, plate


def solution(mesh):
    sizes = tuple(mesh.shape[a] for a in ("lat", "lon", "rad"))
    field = P(None, "rad", "lat", "lon")
    return jax.shard_map(
        functools.partial(on_device, sizes),
        mesh=mesh,
        in_specs=(field, field, P("rad", "lat", "lon"), P("lat", "lon")),
        out_specs=(field, P(None, None, "lat", "lon"), P(None, "lat", "lon")),
        check_vma=False,
    )
```

```python
import functools
import math

import jax
import jax.numpy as jnp
from jax import lax
from jax.experimental import pallas as pl
from jax.experimental.pallas import tpu as pltpu
from jax.sharding import PartitionSpec as P

SWEEPS = 3
PLATES = 12
FACE = 8
RELAX = 0.8
COMPS = 3
LANES = 128
SLOT = 32
MESH = pl.DeviceIdType.MESH
HIGHEST = lax.Precision.HIGHEST
UNROLL = 4


def harmonic(own, other):
    return 2.0 * own * other / (own + other)


def kernel(
    sizes, vel, forc, visc, ids_in,
    last, coarse, plate,
    early, ids, f, eta, w_lat, w_lon, w_rad, gain, diag,
    face_out, face_in, col_out, col_in, pairs,
    lat_sums, lon_sums, stage_out,
    load_sem, send_sem, recv_sem, s1_send, s1_recv, s2_send, s2_recv, g_send, g_recv,
):
    n_lat, n_lon, n_rad = sizes
    n_r, n_a, n_o = visc.shape
    me_lat, me_lon, me_rad = (lax.axis_index(a) for a in ("lat", "lon", "rad"))
    lat_lo, lat_hi = me_lat > 0, me_lat < n_lat - 1
    rad_lo, rad_hi = me_rad > 0, me_rad < n_rad - 1
    lon_up, lon_dn = lax.rem(me_lon + 1, n_lon), lax.rem(me_lon + n_lon - 1, n_lon)
    is_top = me_rad == n_rad - 1
    v = [early.at[t] for t in range(SWEEPS)] + [last]

    loads = [
        pltpu.make_async_copy(visc, eta.at[pl.ds(1, n_r)], load_sem.at[0]),
        pltpu.make_async_copy(vel, v[0].at[:, pl.ds(1, n_r)], load_sem.at[1]),
        pltpu.make_async_copy(forc, f, load_sem.at[2]),
        pltpu.make_async_copy(ids_in, ids, load_sem.at[3]),
    ]
    for load in loads:
        load.start()

    barrier = pltpu.get_barrier_semaphore()

    def greet(device):
        pl.semaphore_signal(barrier, inc=1, device_id=device, device_id_type=MESH)

    expected = 2
    greet({"lon": lon_up})
    greet({"lon": lon_dn})
    for has, device in (
        (lat_lo, {"lat": me_lat - 1}), (lat_hi, {"lat": me_lat + 1}),
        (rad_lo, {"rad": me_rad - 1}), (rad_hi, {"rad": me_rad + 1}),
    ):
        pl.when(has)(functools.partial(greet, device))
        expected = expected + jnp.where(has, 1, 0)
    if n_lat - 1 > SWEEPS + 1:
        for step in range(1, n_lat):
            greet({"lat": lax.rem(me_lat + step, n_lat)})
        expected = expected + (n_lat - 1)
    if n_lon // 2 + n_rad - 1 > SWEEPS + 1:
        for step in range(1, n_lon * n_rad):
            greet({
                "lon": lax.rem(me_lon + step // n_rad, n_lon),
                "rad": lax.rem(me_rad + step % n_rad, n_rad),
            })
        expected = expected + (n_lon * n_rad - 1)

    lane_wide = lax.broadcasted_iota(jnp.int32, (n_a, n_o), 1)
    lane = lax.broadcasted_iota(jnp.int32, (n_a, LANES), 1)
    row = lax.broadcasted_iota(jnp.int32, (n_a, n_o), 0)
    reps = n_o // LANES

    zero_plane = jnp.zeros((n_a, n_o), jnp.float32)
    for has, slot in ((rad_lo, 0), (rad_hi, n_r + 1)):
        @pl.when(jnp.logical_not(has))
        def _():
            eta[slot] = zero_plane
            for t in range(SWEEPS + 1):
                for c in range(COMPS):
                    v[t][c, slot] = zero_plane
    for has, side in ((lat_lo, 0), (lat_hi, 1)):
        @pl.when(jnp.logical_not(has))
        def _():
            for t in range(SWEEPS + 1):
                face_in[t, side] = jnp.zeros(face_in.shape[2:], jnp.float32)

    def links(t):
        rows = pl.ds(0, ((COMPS + 1) if t == 0 else COMPS) * n_r)

        def remote(src, dst, k, device):
            return pltpu.make_async_remote_copy(
                src, dst, send_sem.at[t, k], recv_sem.at[t, k], device_id=device, device_id_type=MESH
            )

        out = [
            (remote(face_out.at[t, 1, rows], face_in.at[t, 0, rows], 0, {"lat": me_lat + 1}), lat_hi, lat_lo),
            (remote(face_out.at[t, 0, rows], face_in.at[t, 1, rows], 1, {"lat": me_lat - 1}), lat_lo, lat_hi),
            (remote(col_out.at[t, 1], col_in.at[t, 0], 2, {"lon": lon_up}), None, None),
            (remote(col_out.at[t, 0], col_in.at[t, 1], 3, {"lon": lon_dn}), None, None),
            (remote(v[t].at[:, n_r], v[t].at[:, 0], 4, {"rad": me_rad + 1}), rad_hi, rad_lo),
            (remote(v[t].at[:, 1], v[t].at[:, n_r + 1], 5, {"rad": me_rad - 1}), rad_lo, rad_hi),
        ]
        if t == 0:
            out += [
                (remote(eta.at[n_r], eta.at[0], 6, {"rad": me_rad + 1}), rad_hi, rad_lo),
                (remote(eta.at[1], eta.at[n_r + 1], 7, {"rad": me_rad - 1}), rad_lo, rad_hi),
            ]
        return out

    def guarded(cond, call):
        if cond is None:
            call()
        else:
            pl.when(cond)(call)

    def start(t):
        for copy, sends, _ in links(t):
            guarded(sends, copy.start)

    def arrive(t):
        for copy, _, receives in links(t):
            guarded(receives, copy.wait_recv)

    def sent(t):
        for copy, sends, _ in links(t):
            guarded(sends, copy.wait_send)

    def pack(t, k, tile, cols):
        face_out[t, 0, k] = tile[:1]
        face_out[t, 1, k] = tile[n_a - 1 :]
        low, high = cols
        hit = lane == k
        low = jnp.where(hit, pltpu.roll(tile[:, :LANES], k, 1), low)
        high = jnp.where(hit, pltpu.roll(tile[:, n_o - LANES :], lax.rem(k + 1, LANES), 1), high)
        return low, high

    def over_radius(body, init, after_top=None):
        def block(i, carry):
            for j in range(UNROLL):
                carry = body(i * UNROLL + j, carry)
            return carry

        count = n_r // UNROLL
        if after_top is not None:
            count = count - 1
            init = block(count, init)
            after_top()
        return lax.fori_loop(0, count, block, init)

    no_cols = (jnp.zeros((n_a, LANES), jnp.float32),) * 2

    def shifted(t, k, tile, cols):
        col_lo, col_hi = cols
        below = jnp.where(row == 0, face_in[t, 0, k], pltpu.roll(tile, 1, 0))
        above = jnp.where(row == n_a - 1, face_in[t, 1, k], pltpu.roll(tile, n_a - 1, 0))
        from_lo = pltpu.roll(col_lo, lax.rem(LANES - k, LANES), 1)
        from_hi = pltpu.roll(col_hi, LANES - 1 - k, 1)
        west = jnp.where(lane_wide == 0, jnp.concatenate([from_lo] * reps, 1), pltpu.roll(tile, 1, 1))
        east = jnp.where(
            lane_wide == n_o - 1, jnp.concatenate([from_hi] * reps, 1), pltpu.roll(tile, n_o - 1, 1)
        )
        return below, above, west, east

    loads[0].wait()
    loads[1].wait()

    def pack_first(r, cols):
        for c in range(COMPS):
            cols = pack(0, c * n_r + r, v[0][c, r + 1], cols)
        return pack(0, COMPS * n_r + r, eta[r + 1], cols)

    low, high = over_radius(pack_first, no_cols)
    col_out[0, 0] = low
    col_out[0, 1] = high
    pl.semaphore_wait(barrier, expected)
    start(0)

    loads[3].wait()
    lat_cell = (me_lat * n_a + row).astype(jnp.float32)
    lon_cell = (me_lon * n_o + lane_wide).astype(jnp.float32)
    phi = math.pi * ((lat_cell + 0.5) / (n_lat * n_a) - 0.5)
    lam = (2.0 * math.pi) * (lon_cell[:1] + 0.5) / (n_lon * n_o)
    cos_lat = jnp.cos(phi)
    rx = cos_lat * jnp.cos(lam)
    ry = cos_lat * jnp.sin(lam)
    rz = jnp.sin(phi)
    blocks = ids.shape[1]
    spread_rows = lax.broadcasted_iota(jnp.int32, (blocks, n_o), 0)
    spread_cols = lax.broadcasted_iota(jnp.int32, (blocks, n_o), 1)
    spread = (spread_cols // FACE == spread_rows).astype(jnp.float32)
    numbers = lax.broadcasted_iota(jnp.int32, (SLOT, n_o), 0)
    onehots = []
    for band in range(n_a // FACE):
        own = jnp.broadcast_to(ids[band : band + 1].astype(jnp.float32), (8, blocks))
        cells = jnp.dot(own, spread, precision=HIGHEST)[:1]
        onehots.append((jnp.abs(cells - numbers.astype(jnp.float32)) < 0.5).astype(jnp.float32))

    arrive(0)

    cols_first = (col_in[0, 0], col_in[0, 1])
    w_rad[0] = harmonic(eta[1], eta[0])

    def weigh(r, carry):
        own = eta[r + 1]
        near = shifted(0, COMPS * n_r + r, own, cols_first)
        below, above, west, east = (harmonic(own, other) for other in near)
        up = harmonic(own, eta[r + 2])
        w_lat[0, r] = below
        w_lat[1, r] = above
        w_lon[0, r] = west
        w_lon[1, r] = east
        w_rad[r + 1] = up
        d = 0.5 * own + (below + above) + (west + east) + (up + w_rad[r])
        diag[r] = d
        gain[r] = RELAX / d
        return carry

    over_radius(weigh, 0)
    loads[2].wait()

    def flux(t, c, r, cols):
        tile = v[t][c, r + 1]
        below, above, west, east = shifted(t, c * n_r + r, tile, cols)
        total = (
            (w_lat[0, r] * below + w_lat[1, r] * above)
            + (w_lon[0, r] * west + w_lon[1, r] * east)
            + (w_rad[r] * v[t][c, r] + w_rad[r + 1] * v[t][c, r + 2])
        )
        return tile, f[c, r] + total

    def s1_copy(step):
        return pltpu.make_async_remote_copy(
            stage_out.at[0], lat_sums.at[me_lat], s1_send.at[step - 1], s1_recv.at[me_lat],
            device_id={"lat": lax.rem(me_lat + step, n_lat)}, device_id_type=MESH,
        )

    def s2_copy(step):
        return pltpu.make_async_remote_copy(
            stage_out.at[1], lon_sums.at[me_lon], s2_send.at[step - 1], s2_recv.at[me_lon],
            device_id={
                "lon": lax.rem(me_lon + step // n_rad, n_lon),
                "rad": lax.rem(me_rad + step % n_rad, n_rad),
            },
            device_id_type=MESH,
        )

    def received(buffer, sem, index):
        pltpu.make_async_remote_copy(
            stage_out.at[0], buffer.at[index], s1_send.at[0], sem.at[index],
            device_id={"lon": lon_up}, device_id_type=MESH,
        ).wait_recv()

    def torques():
        drag = [eta[n_r] * (last[c, n_r] - last[c, n_r - 1]) for c in range(COMPS)]
        twist = (
            (ry * drag[2] - rz * drag[1]) * cos_lat,
            (rz * drag[0] - rx * drag[2]) * cos_lat,
            (rx * drag[1] - ry * drag[0]) * cos_lat,
            cos_lat,
        )
        packed = jnp.zeros((1, LANES), jnp.float32)
        for band in range(n_a // FACE):
            cut = slice(band * FACE, (band + 1) * FACE)
            rows = jnp.concatenate(
                [jnp.sum(x[cut], axis=0, keepdims=True) for x in twist]
                + [jnp.zeros((4, n_o), jnp.float32)], 0,
            )
            sums = lax.dot_general(
                rows, onehots[band], (((1,), (1,)), ((), ())), precision=HIGHEST,
                preferred_element_type=jnp.float32,
            )
            packed = packed + jnp.concatenate([sums[i : i + 1] for i in range(COMPS + 1)], 1)
        stage_out[0] = packed
        lat_sums[me_lat] = packed
        for step in range(1, n_lat):
            s1_copy(step).start()

    for t in range(SWEEPS):
        if t > 0:
            arrive(t)
        cols_in = (col_in[t, 0], col_in[t, 1])

        def sweep(r, cols):
            for c in range(COMPS):
                tile, total = flux(t, c, r, cols_in)
                fresh = (1.0 - RELAX) * tile + gain[r] * total
                v[t + 1][c, r + 1] = fresh
                cols = pack(t + 1, c * n_r + r, fresh, cols)
            return cols

        after_top = (lambda: pl.when(is_top)(torques)) if t == SWEEPS - 1 else None
        low, high = over_radius(sweep, no_cols, after_top)
        col_out[t + 1, 0] = low
        col_out[t + 1, 1] = high
        start(t + 1)

    @pl.when(is_top)
    def _():
        for step in range(1, n_lat):
            received(lat_sums, s1_recv, lax.rem(me_lat + step, n_lat))
        total = lat_sums[0]
        for i in range(1, n_lat):
            total = total + lat_sums[i]
        stage_out[1] = total
        lon_sums[me_lon] = total
        for step in range(1, n_lon * n_rad):
            s2_copy(step).start()

    arrive(SWEEPS)
    cols_in = (col_in[SWEEPS, 0], col_in[SWEEPS, 1])

    def remain(q, carry):
        for c in range(COMPS):
            two = jnp.zeros((n_a, n_o), jnp.float32)
            for s in range(2):
                r = 2 * q + s
                tile, total = flux(SWEEPS, c, r, cols_in)
                two = two + (total - diag[r] * tile)
            at = pl.ds(pl.multiple_of((c * (n_r // 2) + q) * n_a, n_a), n_a)
            for h in range(reps):
                pairs[h, at] = two[:, h * LANES : (h + 1) * LANES]
        return carry

    def remain_block(i, carry):
        for j in range(2):
            carry = remain(2 * i + j, carry)
        return carry

    lax.fori_loop(0, n_r // 4, remain_block, 0)
    half = n_o // 2
    thin_r = lax.broadcasted_iota(jnp.int32, (LANES, half), 0)
    thin_c = lax.broadcasted_iota(jnp.int32, (LANES, half), 1)
    count = COMPS * (n_r // 2) * n_a // 2
    merged = jnp.zeros((count, half), jnp.float32)
    for h in range(reps):
        pick = jnp.where((thin_r + h * LANES) // 2 == thin_c, 0.125, 0.0).astype(jnp.bfloat16)
        both = pairs[h, pl.ds(0, count, stride=2)] + pairs[h, pl.ds(1, count, stride=2)]
        big = both.astype(jnp.bfloat16)
        small = (both - big.astype(jnp.float32)).astype(jnp.bfloat16)
        merged = merged + (
            jnp.dot(big, pick, preferred_element_type=jnp.float32)
            + jnp.dot(small, pick, preferred_element_type=jnp.float32)
        )
    mine = count // COMPS
    spot = pl.ds(pl.multiple_of(me_rad * mine, mine), mine)
    for c in range(COMPS):
        coarse[c, spot] = merged[c * mine : (c + 1) * mine]

    def g_copy(step):
        return pltpu.make_async_remote_copy(
            coarse.at[:, spot], coarse.at[:, spot], g_send.at[step - 1], g_recv.at[me_rad],
            device_id={"rad": lax.rem(me_rad + step, n_rad)}, device_id_type=MESH,
        )

    for step in range(1, n_rad):
        g_copy(step).start()

    for i in range(n_lon):
        @pl.when(jnp.logical_or(jnp.logical_not(is_top), me_lon != i))
        def _():
            received(lon_sums, s2_recv, i)
    total = lon_sums[0]
    for i in range(1, n_lon):
        total = total + lon_sums[i]
    area = total[:, COMPS * SLOT : (COMPS + 1) * SLOT]
    valid = lax.broadcasted_iota(jnp.int32, (1, SLOT), 1) < PLATES
    root = jnp.sqrt(jnp.where(valid, area, 1.0))
    turns = jnp.concatenate(
        [total[:, i * SLOT : (i + 1) * SLOT] / root for i in range(COMPS)]
        + [jnp.zeros((8 - COMPS, SLOT), jnp.float32)], 0,
    )
    for band in range(n_a // FACE):
        cut = slice(band * FACE, (band + 1) * FACE)
        cell = jnp.dot(turns, onehots[band], precision=HIGHEST, preferred_element_type=jnp.float32)
        ox, oy, oz = (cell[i : i + 1] for i in range(COMPS))
        plate[0, cut] = oy * rz[cut] - oz * ry[cut]
        plate[1, cut] = oz * rx[cut] - ox * rz[cut]
        plate[2, cut] = ox * ry[cut] - oy * rx[cut]

    for t in range(SWEEPS + 1):
        sent(t)

    @pl.when(is_top)
    def _():
        for step in range(1, n_lat):
            s1_copy(step).wait_send()
        for step in range(1, n_lon * n_rad):
            s2_copy(step).wait_send()

    for step in range(1, n_rad):
        source = lax.rem(me_rad + step, n_rad)
        region = coarse.at[:, pl.ds(pl.multiple_of(source * mine, mine), mine)]
        pltpu.make_async_remote_copy(
            region, region, g_send.at[0], g_recv.at[source],
            device_id={"rad": source}, device_id_type=MESH,
        ).wait_recv()
        g_copy(step).wait_send()


def write_out(last, coarse, plate, new_v_out, coarse_out, plate_out, sem):
    n_r = new_v_out.shape[1]
    copies = [
        pltpu.make_async_copy(last.at[:, pl.ds(1, n_r)], new_v_out, sem.at[0]),
        pltpu.make_async_copy(coarse, coarse_out, sem.at[1]),
        pltpu.make_async_copy(plate, plate_out, sem.at[2]),
    ]
    for copy in copies:
        copy.start()
    for copy in copies:
        copy.wait()


def on_device(sizes, velocity, forcing, viscosity, plate_ids):
    n_lat, n_lon, n_rad = sizes
    _, n_r, n_a, n_o = velocity.shape
    rounds = SWEEPS + 1
    f32 = jnp.float32
    dma = pltpu.SemaphoreType.DMA
    in_any = pl.BlockSpec(memory_space=pl.ANY)
    in_vmem = pl.BlockSpec(memory_space=pltpu.VMEM)
    coarse_rows = n_rad * (n_r // 2) * (n_a // 2)
    held = pl.pallas_call(
        functools.partial(kernel, sizes),
        out_shape=(
            pltpu.VMEM((COMPS, n_r + 2, n_a, n_o), f32),
            pltpu.VMEM((COMPS, coarse_rows, n_o // 2), f32),
            pltpu.VMEM((COMPS, n_a, n_o), f32),
        ),
        in_specs=[pl.BlockSpec(memory_space=pltpu.HBM)] * 4,
        out_specs=(in_vmem,) * 3,
        scratch_shapes=[
            pltpu.VMEM((SWEEPS, COMPS, n_r + 2, n_a, n_o), f32),
            pltpu.VMEM(plate_ids.shape, jnp.int32),
            pltpu.VMEM((COMPS, n_r, n_a, n_o), f32),
            pltpu.VMEM((n_r + 2, n_a, n_o), f32),
            pltpu.VMEM((2, n_r, n_a, n_o), f32),
            pltpu.VMEM((2, n_r, n_a, n_o), f32),
            pltpu.VMEM((n_r + 1, n_a, n_o), f32),
            pltpu.VMEM((n_r, n_a, n_o), f32),
            pltpu.VMEM((n_r, n_a, n_o), f32),
            pltpu.VMEM((rounds, 2, (COMPS + 1) * n_r, 1, n_o), f32),
            pltpu.VMEM((rounds, 2, (COMPS + 1) * n_r, 1, n_o), f32),
            pltpu.VMEM((rounds, 2, n_a, LANES), f32),
            pltpu.VMEM((rounds, 2, n_a, LANES), f32),
            pltpu.VMEM((n_o // LANES, COMPS * (n_r // 2) * n_a, LANES), f32),
            pltpu.VMEM((n_lat, 1, LANES), f32),
            pltpu.VMEM((n_lon, 1, LANES), f32),
            pltpu.VMEM((2, 1, LANES), f32),
            dma((4,)),
            dma((rounds, 8)),
            dma((rounds, 8)),
            dma((n_lat,)),
            dma((n_lat,)),
            dma((n_lon * n_rad,)),
            dma((n_lon,)),
            dma((n_rad,)),
            dma((n_rad,)),
        ],
        compiler_params=pltpu.CompilerParams(
            collective_id=0, has_side_effects=True, vmem_limit_bytes=24 * 2**20
        ),
    )(*(
        pltpu.with_memory_space_constraint(x, pltpu.HBM)
        for x in (velocity, forcing, viscosity, plate_ids)
    ))
    new_v, coarse, plate = pl.pallas_call(
        write_out,
        out_shape=(
            jax.ShapeDtypeStruct(velocity.shape, f32),
            jax.ShapeDtypeStruct((COMPS, coarse_rows, n_o // 2), f32),
            jax.ShapeDtypeStruct((COMPS, n_a, n_o), f32),
        ),
        in_specs=[in_vmem] * 3,
        out_specs=(in_any,) * 3,
        scratch_shapes=[dma((3,))],
        compiler_params=pltpu.CompilerParams(vmem_limit_bytes=4 * 2**20),
    )(*(pltpu.with_memory_space_constraint(x, pltpu.VMEM) for x in held))
    coarse = coarse.reshape(COMPS, n_rad * (n_r // 2), n_a // 2, n_o // 2)
    return new_v, coarse, plate


def solution(mesh):
    sizes = tuple(mesh.shape[a] for a in ("lat", "lon", "rad"))
    field = P(None, "rad", "lat", "lon")
    return jax.shard_map(
        functools.partial(on_device, sizes),
        mesh=mesh,
        in_specs=(field, field, P("rad", "lat", "lon"), P("lat", "lon")),
        out_specs=(field, P(None, None, "lat", "lon"), P(None, "lat", "lon")),
        check_vma=False,
    )
```

```python
import functools
import math

import jax
import jax.numpy as jnp
from jax import lax
from jax.experimental import pallas as pl
from jax.experimental.pallas import tpu as pltpu
from jax.sharding import PartitionSpec as P

SWEEPS = 3
PLATES = 12
FACE = 8
RELAX = 0.8
COMPS = 3
LANES = 128
SLOT = 32
MESH = pl.DeviceIdType.MESH
HIGHEST = lax.Precision.HIGHEST
UNROLL = 4


def harmonic(own, other):
    return 2.0 * own * other / (own + other)


class Link:
    def __init__(self, make):
        self.make = make

    def start(self):
        self.make().start()

    def wait_send(self):
        self.make().wait_send()

    def wait_recv(self):
        self.make().wait_recv()


def kernel(
    sizes, vel, forc, visc, ids_in,
    last, coarse, plate,
    early, ids, f, eta, w_lat, w_lon, w_rad, gain, diag,
    face_out, face_in, col_out, col_in, pairs,
    lat_sums, lon_sums, stage_out,
    load_sem, send_sem, recv_sem, s1_send, s1_recv, s2_send, s2_recv, g_send, g_recv,
):
    n_lat, n_lon, n_rad = sizes
    n_r, n_a, n_o = visc.shape
    me_lat, me_lon, me_rad = (lax.axis_index(a) for a in ("lat", "lon", "rad"))
    lat_lo, lat_hi = me_lat > 0, me_lat < n_lat - 1
    rad_lo, rad_hi = me_rad > 0, me_rad < n_rad - 1
    lon_up, lon_dn = lax.rem(me_lon + 1, n_lon), lax.rem(me_lon + n_lon - 1, n_lon)
    is_top = me_rad == n_rad - 1
    v = [early.at[t] for t in range(SWEEPS)] + [last]

    barrier = pltpu.get_barrier_semaphore()

    def greet(device):
        pl.semaphore_signal(barrier, inc=1, device_id=device, device_id_type=MESH)

    expected = 2
    greet({"lon": lon_up})
    greet({"lon": lon_dn})
    for has, device in (
        (lat_lo, {"lat": me_lat - 1}), (lat_hi, {"lat": me_lat + 1}),
        (rad_lo, {"rad": me_rad - 1}), (rad_hi, {"rad": me_rad + 1}),
    ):
        pl.when(has)(functools.partial(greet, device))
        expected = expected + jnp.where(has, 1, 0)
    if n_lat - 1 > SWEEPS + 1:
        for step in range(1, n_lat):
            greet({"lat": lax.rem(me_lat + step, n_lat)})
        expected = expected + (n_lat - 1)
    if n_lon // 2 + n_rad - 1 > SWEEPS + 1:
        for step in range(1, n_lon * n_rad):
            greet({
                "lon": lax.rem(me_lon + step // n_rad, n_lon),
                "rad": lax.rem(me_rad + step % n_rad, n_rad),
            })
        expected = expected + (n_lon * n_rad - 1)

    loads = [
        pltpu.make_async_copy(visc, eta.at[pl.ds(1, n_r)], load_sem.at[0]),
        pltpu.make_async_copy(vel, v[0].at[:, pl.ds(1, n_r)], load_sem.at[1]),
        pltpu.make_async_copy(forc, f, load_sem.at[2]),
        pltpu.make_async_copy(ids_in, ids, load_sem.at[3]),
    ]
    for load in loads:
        load.start()

    lane_wide = lax.broadcasted_iota(jnp.int32, (n_a, n_o), 1)
    lane = lax.broadcasted_iota(jnp.int32, (n_a, LANES), 1)
    row = lax.broadcasted_iota(jnp.int32, (n_a, n_o), 0)
    reps = n_o // LANES

    zero_plane = jnp.zeros((n_a, n_o), jnp.float32)
    for has, slot in ((rad_lo, 0), (rad_hi, n_r + 1)):
        @pl.when(jnp.logical_not(has))
        def _():
            eta[slot] = zero_plane
            for t in range(SWEEPS + 1):
                for c in range(COMPS):
                    v[t][c, slot] = zero_plane
    for has, side in ((lat_lo, 0), (lat_hi, 1)):
        @pl.when(jnp.logical_not(has))
        def _():
            for t in range(SWEEPS + 1):
                face_in[t, side] = jnp.zeros(face_in.shape[2:], jnp.float32)

    blocks_r = n_r // UNROLL
    order = [blocks_r - 1] + list(range(blocks_r - 1))

    def chunk(t, b):
        comps = COMPS + 1 if t == 0 else COMPS
        rows = pl.ds(b * UNROLL * comps, UNROLL * comps)

        def remote(src, dst, k, device):
            return Link(functools.partial(
                pltpu.make_async_remote_copy,
                src, dst, send_sem.at[t, b, k], recv_sem.at[t, b, k],
                device_id=device, device_id_type=MESH,
            ))

        sends = [
            (remote(col_out.at[t, b, 1], col_in.at[t, b, 0], 2, {"lon": lon_up}), None),
            (remote(col_out.at[t, b, 0], col_in.at[t, b, 1], 3, {"lon": lon_dn}), None),
            (remote(face_out.at[t, 1, rows], face_in.at[t, 0, rows], 0, {"lat": me_lat + 1}), lat_hi),
            (remote(face_out.at[t, 0, rows], face_in.at[t, 1, rows], 1, {"lat": me_lat - 1}), lat_lo),
        ]
        takes = [None, None, lat_lo, lat_hi]
        ups = [(remote(v[t].at[:, n_r], v[t].at[:, 0], 4, {"rad": me_rad + 1}), rad_hi)]
        downs = [(remote(v[t].at[:, 1], v[t].at[:, n_r + 1], 5, {"rad": me_rad - 1}), rad_lo)]
        if t == 0:
            ups.append((remote(eta.at[n_r], eta.at[0], 6, {"rad": me_rad + 1}), rad_hi))
            downs.append((remote(eta.at[1], eta.at[n_r + 1], 7, {"rad": me_rad - 1}), rad_lo))
        return sends, takes, ups, downs

    def guarded(cond, call):
        if cond is None:
            call()
        else:
            pl.when(cond)(call)

    def start(t, b):
        sends, _, _, _ = chunk(t, b)
        for copy, cond in sends:
            guarded(cond, copy.start)
        if b == blocks_r - 1:
            for copy, cond in chunk(t, 0)[2]:
                guarded(cond, copy.start)
        if b == 0:
            for copy, cond in chunk(t, 0)[3]:
                guarded(cond, copy.start)

    def arrive(t, b):
        sends, takes, _, _ = chunk(t, b)
        _, _, ups, downs = chunk(t, 0)
        if b == 0:
            for copy, _ in ups:
                guarded(rad_lo, copy.wait_recv)
        if b == blocks_r - 1:
            for copy, _ in downs:
                guarded(rad_hi, copy.wait_recv)
        for (copy, _), cond in zip(sends, takes):
            guarded(cond, copy.wait_recv)

    def sent(t):
        for b in range(blocks_r):
            for copy, cond in chunk(t, b)[0]:
                guarded(cond, copy.wait_send)
        _, _, ups, downs = chunk(t, 0)
        for copy, cond in ups + downs:
            guarded(cond, copy.wait_send)

    def lane_of(t, j, c):
        return j * (COMPS + 1 if t == 0 else COMPS) + c

    def row_of(t, r, c):
        return r * (COMPS + 1 if t == 0 else COMPS) + c

    def pack(t, b, j, c, tile, cols):
        face_out[t, 0, row_of(t, b * UNROLL + j, c)] = tile[:1]
        face_out[t, 1, row_of(t, b * UNROLL + j, c)] = tile[n_a - 1 :]
        k = lane_of(t, j, c)
        low, high = cols
        hit = lane == k
        low = jnp.where(hit, pltpu.roll(tile[:, :LANES], k, 1) if k else tile[:, :LANES], low)
        high = jnp.where(hit, pltpu.roll(tile[:, n_o - LANES :], (k + 1) % LANES, 1), high)
        return low, high

    def put_cols(t, b, cols):
        col_out[t, b, 0], col_out[t, b, 1] = cols

    no_cols = (jnp.zeros((n_a, LANES), jnp.float32),) * 2

    def shifted(t, b, j, c, tile, cols):
        col_lo, col_hi = cols
        k = lane_of(t, j, c)
        at = row_of(t, b * UNROLL + j, c)
        below = jnp.where(row == 0, face_in[t, 0, at], pltpu.roll(tile, 1, 0))
        above = jnp.where(row == n_a - 1, face_in[t, 1, at], pltpu.roll(tile, n_a - 1, 0))
        from_lo = pltpu.roll(col_lo, LANES - k, 1) if k else col_lo
        from_hi = pltpu.roll(col_hi, LANES - 1 - k, 1)
        west = jnp.where(lane_wide == 0, jnp.concatenate([from_lo] * reps, 1), pltpu.roll(tile, 1, 1))
        east = jnp.where(
            lane_wide == n_o - 1, jnp.concatenate([from_hi] * reps, 1), pltpu.roll(tile, n_o - 1, 1)
        )
        return below, above, west, east

    loads[0].wait()
    loads[1].wait()
    for b in order:
        cols = no_cols
        for j in range(UNROLL):
            r = b * UNROLL + j
            for c in range(COMPS):
                cols = pack(0, b, j, c, v[0][c, r + 1], cols)
            cols = pack(0, b, j, COMPS, eta[r + 1], cols)
        put_cols(0, b, cols)
    pl.semaphore_wait(barrier, expected)
    for b in order:
        start(0, b)

    loads[3].wait()
    lat_cell = (me_lat * n_a + row).astype(jnp.float32)
    lon_cell = (me_lon * n_o + lane_wide).astype(jnp.float32)
    phi = math.pi * ((lat_cell + 0.5) / (n_lat * n_a) - 0.5)
    lam = (2.0 * math.pi) * (lon_cell[:1] + 0.5) / (n_lon * n_o)
    cos_lat = jnp.cos(phi)
    rx = cos_lat * jnp.cos(lam)
    ry = cos_lat * jnp.sin(lam)
    rz = jnp.sin(phi)
    blocks = ids.shape[1]
    spread_rows = lax.broadcasted_iota(jnp.int32, (blocks, n_o), 0)
    spread_cols = lax.broadcasted_iota(jnp.int32, (blocks, n_o), 1)
    spread = (spread_cols // FACE == spread_rows).astype(jnp.float32)
    numbers = lax.broadcasted_iota(jnp.int32, (SLOT, n_o), 0)
    onehots = []
    for band in range(n_a // FACE):
        own = jnp.broadcast_to(ids[band : band + 1].astype(jnp.float32), (8, blocks))
        cells = jnp.dot(own, spread, precision=HIGHEST)[:1]
        onehots.append((jnp.abs(cells - numbers.astype(jnp.float32)) < 0.5).astype(jnp.float32))

    def weigh(b, cols):
        for j in range(UNROLL):
            r = b * UNROLL + j
            own = eta[r + 1]
            near = shifted(0, b, j, COMPS, own, cols)
            below, above, west, east = (harmonic(own, other) for other in near)
            down = harmonic(own, eta[r]) if j == 0 else up
            up = harmonic(own, eta[r + 2])
            w_lat[0, r] = below
            w_lat[1, r] = above
            w_lon[0, r] = west
            w_lon[1, r] = east
            w_rad[r] = down
            w_rad[r + 1] = up
            d = 0.5 * own + (below + above) + (west + east) + (up + down)
            diag[r] = d
            gain[r] = RELAX / d

    def flux(t, b, j, c, cols):
        r = b * UNROLL + j
        tile = v[t][c, r + 1]
        below, above, west, east = shifted(t, b, j, c, tile, cols)
        total = (
            (w_lat[0, r] * below + w_lat[1, r] * above)
            + (w_lon[0, r] * west + w_lon[1, r] * east)
            + (w_rad[r] * v[t][c, r] + w_rad[r + 1] * v[t][c, r + 2])
        )
        return tile, f[c, r] + total

    def s1_copy(step):
        return pltpu.make_async_remote_copy(
            stage_out.at[0], lat_sums.at[me_lat], s1_send.at[step - 1], s1_recv.at[me_lat],
            device_id={"lat": lax.rem(me_lat + step, n_lat)}, device_id_type=MESH,
        )

    def s2_copy(step):
        return pltpu.make_async_remote_copy(
            stage_out.at[1], lon_sums.at[me_lon], s2_send.at[step - 1], s2_recv.at[me_lon],
            device_id={
                "lon": lax.rem(me_lon + step // n_rad, n_lon),
                "rad": lax.rem(me_rad + step % n_rad, n_rad),
            },
            device_id_type=MESH,
        )

    def received(buffer, sem, index):
        pltpu.make_async_remote_copy(
            stage_out.at[0], buffer.at[index], s1_send.at[0], sem.at[index],
            device_id={"lon": lon_up}, device_id_type=MESH,
        ).wait_recv()

    def torques():
        drag = [eta[n_r] * (last[c, n_r] - last[c, n_r - 1]) for c in range(COMPS)]
        twist = (
            (ry * drag[2] - rz * drag[1]) * cos_lat,
            (rz * drag[0] - rx * drag[2]) * cos_lat,
            (rx * drag[1] - ry * drag[0]) * cos_lat,
            cos_lat,
        )
        packed = jnp.zeros((1, LANES), jnp.float32)
        for band in range(n_a // FACE):
            cut = slice(band * FACE, (band + 1) * FACE)
            rows = jnp.concatenate(
                [jnp.sum(x[cut], axis=0, keepdims=True) for x in twist]
                + [jnp.zeros((4, n_o), jnp.float32)], 0,
            )
            sums = lax.dot_general(
                rows, onehots[band], (((1,), (1,)), ((), ())), precision=HIGHEST,
                preferred_element_type=jnp.float32,
            )
            packed = packed + jnp.concatenate([sums[i : i + 1] for i in range(COMPS + 1)], 1)
        stage_out[0] = packed
        lat_sums[me_lat] = packed
        for step in range(1, n_lat):
            s1_copy(step).start()

    for t in range(SWEEPS):
        for b in order:
            arrive(t, b)
            cols_in = (col_in[t, b, 0], col_in[t, b, 1])
            if t == 0:
                weigh(b, cols_in)
                if b == order[0]:
                    loads[2].wait()
            cols = no_cols
            for j in range(UNROLL):
                r = b * UNROLL + j
                for c in range(COMPS):
                    tile, total = flux(t, b, j, c, cols_in)
                    fresh = (1.0 - RELAX) * tile + gain[r] * total
                    v[t + 1][c, r + 1] = fresh
                    cols = pack(t + 1, b, j, c, fresh, cols)
            put_cols(t + 1, b, cols)
            if t == SWEEPS - 1 and b == blocks_r - 1:
                pl.when(is_top)(torques)
            start(t + 1, b)

    @pl.when(is_top)
    def _():
        for step in range(1, n_lat):
            received(lat_sums, s1_recv, lax.rem(me_lat + step, n_lat))
        total = lat_sums[0]
        for i in range(1, n_lat):
            total = total + lat_sums[i]
        stage_out[1] = total
        lon_sums[me_lon] = total
        for step in range(1, n_lon * n_rad):
            s2_copy(step).start()

    for b in order:
        arrive(SWEEPS, b)
        cols_in = (col_in[SWEEPS, b, 0], col_in[SWEEPS, b, 1])
        for i in range(UNROLL // 2):
            for c in range(COMPS):
                two = jnp.zeros((n_a, n_o), jnp.float32)
                for j in (2 * i, 2 * i + 1):
                    tile, total = flux(SWEEPS, b, j, c, cols_in)
                    two = two + (total - diag[b * UNROLL + j] * tile)
                at = pl.ds((c * (n_r // 2) + b * (UNROLL // 2) + i) * n_a, n_a)
                for h in range(reps):
                    pairs[h, at] = two[:, h * LANES : (h + 1) * LANES]
    half = n_o // 2
    thin_r = lax.broadcasted_iota(jnp.int32, (LANES, half), 0)
    thin_c = lax.broadcasted_iota(jnp.int32, (LANES, half), 1)
    count = COMPS * (n_r // 2) * n_a // 2
    merged = jnp.zeros((count, half), jnp.float32)
    for h in range(reps):
        pick = jnp.where((thin_r + h * LANES) // 2 == thin_c, 0.125, 0.0).astype(jnp.bfloat16)
        both = pairs[h, pl.ds(0, count, stride=2)] + pairs[h, pl.ds(1, count, stride=2)]
        big = both.astype(jnp.bfloat16)
        small = (both - big.astype(jnp.float32)).astype(jnp.bfloat16)
        merged = merged + (
            jnp.dot(big, pick, preferred_element_type=jnp.float32)
            + jnp.dot(small, pick, preferred_element_type=jnp.float32)
        )
    mine = count // COMPS
    spot = pl.ds(pl.multiple_of(me_rad * mine, mine), mine)
    for c in range(COMPS):
        coarse[c, spot] = merged[c * mine : (c + 1) * mine]

    def g_copy(step):
        return pltpu.make_async_remote_copy(
            coarse.at[:, spot], coarse.at[:, spot], g_send.at[step - 1], g_recv.at[me_rad],
            device_id={"rad": lax.rem(me_rad + step, n_rad)}, device_id_type=MESH,
        )

    for step in range(1, n_rad):
        g_copy(step).start()

    for i in range(n_lon):
        @pl.when(jnp.logical_or(jnp.logical_not(is_top), me_lon != i))
        def _():
            received(lon_sums, s2_recv, i)
    total = lon_sums[0]
    for i in range(1, n_lon):
        total = total + lon_sums[i]
    area = total[:, COMPS * SLOT : (COMPS + 1) * SLOT]
    valid = lax.broadcasted_iota(jnp.int32, (1, SLOT), 1) < PLATES
    root = jnp.sqrt(jnp.where(valid, area, 1.0))
    turns = jnp.concatenate(
        [total[:, i * SLOT : (i + 1) * SLOT] / root for i in range(COMPS)]
        + [jnp.zeros((8 - COMPS, SLOT), jnp.float32)], 0,
    )
    for band in range(n_a // FACE):
        cut = slice(band * FACE, (band + 1) * FACE)
        cell = jnp.dot(turns, onehots[band], precision=HIGHEST, preferred_element_type=jnp.float32)
        ox, oy, oz = (cell[i : i + 1] for i in range(COMPS))
        plate[0, cut] = oy * rz[cut] - oz * ry[cut]
        plate[1, cut] = oz * rx[cut] - ox * rz[cut]
        plate[2, cut] = ox * ry[cut] - oy * rx[cut]

    for t in range(SWEEPS + 1):
        sent(t)

    @pl.when(is_top)
    def _():
        for step in range(1, n_lat):
            s1_copy(step).wait_send()
        for step in range(1, n_lon * n_rad):
            s2_copy(step).wait_send()

    for step in range(1, n_rad):
        source = lax.rem(me_rad + step, n_rad)
        region = coarse.at[:, pl.ds(pl.multiple_of(source * mine, mine), mine)]
        pltpu.make_async_remote_copy(
            region, region, g_send.at[0], g_recv.at[source],
            device_id={"rad": source}, device_id_type=MESH,
        ).wait_recv()
        g_copy(step).wait_send()


def write_out(last, coarse, plate, new_v_out, coarse_out, plate_out, sem):
    n_r = new_v_out.shape[1]
    copies = [
        pltpu.make_async_copy(last.at[:, pl.ds(1, n_r)], new_v_out, sem.at[0]),
        pltpu.make_async_copy(coarse, coarse_out, sem.at[1]),
        pltpu.make_async_copy(plate, plate_out, sem.at[2]),
    ]
    for copy in copies:
        copy.start()
    for copy in copies:
        copy.wait()


def on_device(sizes, velocity, forcing, viscosity, plate_ids):
    n_lat, n_lon, n_rad = sizes
    _, n_r, n_a, n_o = velocity.shape
    rounds = SWEEPS + 1
    chunks = n_r // UNROLL
    f32 = jnp.float32
    dma = pltpu.SemaphoreType.DMA
    in_any = pl.BlockSpec(memory_space=pl.ANY)
    in_vmem = pl.BlockSpec(memory_space=pltpu.VMEM)
    coarse_rows = n_rad * (n_r // 2) * (n_a // 2)
    held = pl.pallas_call(
        functools.partial(kernel, sizes),
        out_shape=(
            pltpu.VMEM((COMPS, n_r + 2, n_a, n_o), f32),
            pltpu.VMEM((COMPS, coarse_rows, n_o // 2), f32),
            pltpu.VMEM((COMPS, n_a, n_o), f32),
        ),
        in_specs=[pl.BlockSpec(memory_space=pltpu.HBM)] * 4,
        out_specs=(in_vmem,) * 3,
        scratch_shapes=[
            pltpu.VMEM((SWEEPS, COMPS, n_r + 2, n_a, n_o), f32),
            pltpu.VMEM(plate_ids.shape, jnp.int32),
            pltpu.VMEM((COMPS, n_r, n_a, n_o), f32),
            pltpu.VMEM((n_r + 2, n_a, n_o), f32),
            pltpu.VMEM((2, n_r, n_a, n_o), f32),
            pltpu.VMEM((2, n_r, n_a, n_o), f32),
            pltpu.VMEM((n_r + 1, n_a, n_o), f32),
            pltpu.VMEM((n_r, n_a, n_o), f32),
            pltpu.VMEM((n_r, n_a, n_o), f32),
            pltpu.VMEM((rounds, 2, (COMPS + 1) * n_r, 1, n_o), f32),
            pltpu.VMEM((rounds, 2, (COMPS + 1) * n_r, 1, n_o), f32),
            pltpu.VMEM((rounds, chunks, 2, n_a, LANES), f32),
            pltpu.VMEM((rounds, chunks, 2, n_a, LANES), f32),
            pltpu.VMEM((n_o // LANES, COMPS * (n_r // 2) * n_a, LANES), f32),
            pltpu.VMEM((n_lat, 1, LANES), f32),
            pltpu.VMEM((n_lon, 1, LANES), f32),
            pltpu.VMEM((2, 1, LANES), f32),
            dma((4,)),
            dma((rounds, chunks, 8)),
            dma((rounds, chunks, 8)),
            dma((n_lat,)),
            dma((n_lat,)),
            dma((n_lon * n_rad,)),
            dma((n_lon,)),
            dma((n_rad,)),
            dma((n_rad,)),
        ],
        compiler_params=pltpu.CompilerParams(
            collective_id=0, has_side_effects=True, vmem_limit_bytes=24 * 2**20
        ),
    )(*(
        pltpu.with_memory_space_constraint(x, pltpu.HBM)
        for x in (velocity, forcing, viscosity, plate_ids)
    ))
    new_v, coarse, plate = pl.pallas_call(
        write_out,
        out_shape=(
            jax.ShapeDtypeStruct(velocity.shape, f32),
            jax.ShapeDtypeStruct((COMPS, coarse_rows, n_o // 2), f32),
            jax.ShapeDtypeStruct((COMPS, n_a, n_o), f32),
        ),
        in_specs=[in_vmem] * 3,
        out_specs=(in_any,) * 3,
        scratch_shapes=[dma((3,))],
        compiler_params=pltpu.CompilerParams(vmem_limit_bytes=4 * 2**20),
    )(*(pltpu.with_memory_space_constraint(x, pltpu.VMEM) for x in held))
    coarse = coarse.reshape(COMPS, n_rad * (n_r // 2), n_a // 2, n_o // 2)
    return new_v, coarse, plate


def solution(mesh):
    sizes = tuple(mesh.shape[a] for a in ("lat", "lon", "rad"))
    field = P(None, "rad", "lat", "lon")
    return jax.shard_map(
        functools.partial(on_device, sizes),
        mesh=mesh,
        in_specs=(field, field, P("rad", "lat", "lon"), P("lat", "lon")),
        out_specs=(field, P(None, None, "lat", "lon"), P(None, "lat", "lon")),
        check_vma=False,
    )
```

```python
import functools
import math

import jax
import jax.numpy as jnp
from jax import lax
from jax.experimental import pallas as pl
from jax.experimental.pallas import tpu as pltpu
from jax.sharding import PartitionSpec as P

SWEEPS = 3
PLATES = 12
FACE = 8
RELAX = 0.8
COMPS = 3
LANES = 128
SLOT = 32
MESH = pl.DeviceIdType.MESH
HIGHEST = lax.Precision.HIGHEST
UNROLL = 4


def harmonic(own, other):
    return 2.0 * own * other / (own + other)


class Link:
    def __init__(self, make):
        self.make = make

    def start(self):
        self.make().start()

    def wait_send(self):
        self.make().wait_send()

    def wait_recv(self):
        self.make().wait_recv()


def kernel(
    sizes, vel, forc, visc, ids_in,
    last, coarse, plate,
    early, ids, f, eta, w_lat, w_lon, w_rad, gain, diag,
    face_out, face_in, col_out, col_in, pairs,
    lat_sums, lon_sums, stage_out,
    load_sem, send_sem, recv_sem, s1_send, s1_recv, s2_send, s2_recv, g_send, g_recv,
):
    n_lat, n_lon, n_rad = sizes
    n_r, n_a, n_o = visc.shape
    me_lat, me_lon, me_rad = (lax.axis_index(a) for a in ("lat", "lon", "rad"))
    lat_lo, lat_hi = me_lat > 0, me_lat < n_lat - 1
    rad_lo, rad_hi = me_rad > 0, me_rad < n_rad - 1
    lon_up, lon_dn = lax.rem(me_lon + 1, n_lon), lax.rem(me_lon + n_lon - 1, n_lon)
    is_top = me_rad == n_rad - 1
    v = [early.at[t] for t in range(SWEEPS)] + [last]

    barrier = pltpu.get_barrier_semaphore()

    def greet(device):
        pl.semaphore_signal(barrier, inc=1, device_id=device, device_id_type=MESH)

    expected = 2
    greet({"lon": lon_up})
    greet({"lon": lon_dn})
    for has, device in (
        (lat_lo, {"lat": me_lat - 1}), (lat_hi, {"lat": me_lat + 1}),
        (rad_lo, {"rad": me_rad - 1}), (rad_hi, {"rad": me_rad + 1}),
    ):
        pl.when(has)(functools.partial(greet, device))
        expected = expected + jnp.where(has, 1, 0)
    if n_lat - 1 > SWEEPS + 1:
        for step in range(1, n_lat):
            greet({"lat": lax.rem(me_lat + step, n_lat)})
        expected = expected + (n_lat - 1)
    if n_lon // 2 + n_rad - 1 > SWEEPS + 1:
        for step in range(1, n_lon * n_rad):
            greet({
                "lon": lax.rem(me_lon + step // n_rad, n_lon),
                "rad": lax.rem(me_rad + step % n_rad, n_rad),
            })
        expected = expected + (n_lon * n_rad - 1)

    loads = [
        pltpu.make_async_copy(visc, eta.at[pl.ds(1, n_r)], load_sem.at[0]),
        pltpu.make_async_copy(vel, v[0].at[:, pl.ds(1, n_r)], load_sem.at[1]),
        pltpu.make_async_copy(forc, f, load_sem.at[2]),
        pltpu.make_async_copy(ids_in, ids, load_sem.at[3]),
    ]
    for load in loads:
        load.start()

    lane_wide = lax.broadcasted_iota(jnp.int32, (n_a, n_o), 1)
    lane = lax.broadcasted_iota(jnp.int32, (n_a, LANES), 1)
    row = lax.broadcasted_iota(jnp.int32, (n_a, n_o), 0)
    reps = n_o // LANES

    zero_plane = jnp.zeros((n_a, n_o), jnp.float32)
    for has, slot in ((rad_lo, 0), (rad_hi, n_r + 1)):
        @pl.when(jnp.logical_not(has))
        def _():
            eta[slot] = zero_plane
            for t in range(SWEEPS + 1):
                for c in range(COMPS):
                    v[t][c, slot] = zero_plane
    for has, side in ((lat_lo, 0), (lat_hi, 1)):
        @pl.when(jnp.logical_not(has))
        def _():
            for t in range(SWEEPS + 1):
                face_in[t, side] = jnp.zeros(face_in.shape[2:], jnp.float32)

    blocks_r = n_r // UNROLL
    order = [blocks_r - 1] + list(range(blocks_r - 1))

    def chunk(t, b):
        comps = COMPS + 1 if t == 0 else COMPS
        rows = pl.ds(b * UNROLL * comps, UNROLL * comps)

        def remote(src, dst, k, device):
            return Link(functools.partial(
                pltpu.make_async_remote_copy,
                src, dst, send_sem.at[t, b, k], recv_sem.at[t, b, k],
                device_id=device, device_id_type=MESH,
            ))

        sends = [
            (remote(col_out.at[t, b, 1], col_in.at[t, b, 0], 2, {"lon": lon_up}), None),
            (remote(col_out.at[t, b, 0], col_in.at[t, b, 1], 3, {"lon": lon_dn}), None),
            (remote(face_out.at[t, 1, rows], face_in.at[t, 0, rows], 0, {"lat": me_lat + 1}), lat_hi),
            (remote(face_out.at[t, 0, rows], face_in.at[t, 1, rows], 1, {"lat": me_lat - 1}), lat_lo),
        ]
        takes = [None, None, lat_lo, lat_hi]
        ups = [(remote(v[t].at[:, n_r], v[t].at[:, 0], 4, {"rad": me_rad + 1}), rad_hi)]
        downs = [(remote(v[t].at[:, 1], v[t].at[:, n_r + 1], 5, {"rad": me_rad - 1}), rad_lo)]
        if t == 0:
            ups.append((remote(eta.at[n_r], eta.at[0], 6, {"rad": me_rad + 1}), rad_hi))
            downs.append((remote(eta.at[1], eta.at[n_r + 1], 7, {"rad": me_rad - 1}), rad_lo))
        return sends, takes, ups, downs

    def guarded(cond, call):
        if cond is None:
            call()
        else:
            pl.when(cond)(call)

    def start(t, b):
        sends, _, _, _ = chunk(t, b)
        for copy, cond in sends:
            guarded(cond, copy.start)
        if b == blocks_r - 1:
            for copy, cond in chunk(t, 0)[2]:
                guarded(cond, copy.start)
        if b == 0:
            for copy, cond in chunk(t, 0)[3]:
                guarded(cond, copy.start)

    def arrive(t, b):
        sends, takes, _, _ = chunk(t, b)
        _, _, ups, downs = chunk(t, 0)
        if b == 0:
            for copy, _ in ups:
                guarded(rad_lo, copy.wait_recv)
        if b == blocks_r - 1:
            for copy, _ in downs:
                guarded(rad_hi, copy.wait_recv)
        for (copy, _), cond in zip(sends, takes):
            guarded(cond, copy.wait_recv)

    def sent(t):
        for b in range(blocks_r):
            for copy, cond in chunk(t, b)[0]:
                guarded(cond, copy.wait_send)
        _, _, ups, downs = chunk(t, 0)
        for copy, cond in ups + downs:
            guarded(cond, copy.wait_send)

    def lane_of(t, j, c):
        return j * (COMPS + 1 if t == 0 else COMPS) + c

    def row_of(t, r, c):
        return r * (COMPS + 1 if t == 0 else COMPS) + c

    def pack(t, b, j, c, tile, cols):
        face_out[t, 0, row_of(t, b * UNROLL + j, c)] = tile[:1]
        face_out[t, 1, row_of(t, b * UNROLL + j, c)] = tile[n_a - 1 :]
        k = lane_of(t, j, c)
        low, high = cols
        hit = lane == k
        low = jnp.where(hit, pltpu.roll(tile[:, :LANES], k, 1) if k else tile[:, :LANES], low)
        high = jnp.where(hit, pltpu.roll(tile[:, n_o - LANES :], (k + 1) % LANES, 1), high)
        return low, high

    def put_cols(t, b, cols):
        col_out[t, b, 0], col_out[t, b, 1] = cols

    no_cols = (jnp.zeros((n_a, LANES), jnp.float32),) * 2

    def shifted(t, b, j, c, tile, cols):
        col_lo, col_hi = cols
        k = lane_of(t, j, c)
        at = row_of(t, b * UNROLL + j, c)
        below = jnp.where(row == 0, face_in[t, 0, at], pltpu.roll(tile, 1, 0))
        above = jnp.where(row == n_a - 1, face_in[t, 1, at], pltpu.roll(tile, n_a - 1, 0))
        from_lo = pltpu.roll(col_lo, LANES - k, 1) if k else col_lo
        from_hi = pltpu.roll(col_hi, LANES - 1 - k, 1)
        west = jnp.where(lane_wide == 0, jnp.concatenate([from_lo] * reps, 1), pltpu.roll(tile, 1, 1))
        east = jnp.where(
            lane_wide == n_o - 1, jnp.concatenate([from_hi] * reps, 1), pltpu.roll(tile, n_o - 1, 1)
        )
        return below, above, west, east

    loads[0].wait()
    loads[1].wait()
    for b in order:
        cols = no_cols
        for j in range(UNROLL):
            r = b * UNROLL + j
            for c in range(COMPS):
                cols = pack(0, b, j, c, v[0][c, r + 1], cols)
            cols = pack(0, b, j, COMPS, eta[r + 1], cols)
        put_cols(0, b, cols)
    pl.semaphore_wait(barrier, expected)
    for b in order:
        start(0, b)

    loads[3].wait()
    lat_cell = (me_lat * n_a + row).astype(jnp.float32)
    lon_cell = (me_lon * n_o + lane_wide).astype(jnp.float32)
    phi = math.pi * ((lat_cell + 0.5) / (n_lat * n_a) - 0.5)
    lam = (2.0 * math.pi) * (lon_cell[:1] + 0.5) / (n_lon * n_o)
    cos_lat = jnp.cos(phi)
    rx = cos_lat * jnp.cos(lam)
    ry = cos_lat * jnp.sin(lam)
    rz = jnp.sin(phi)
    blocks = ids.shape[1]
    spread_rows = lax.broadcasted_iota(jnp.int32, (blocks, n_o), 0)
    spread_cols = lax.broadcasted_iota(jnp.int32, (blocks, n_o), 1)
    spread = (spread_cols // FACE == spread_rows).astype(jnp.float32)
    numbers = lax.broadcasted_iota(jnp.int32, (SLOT, n_o), 0)
    onehots = []
    for band in range(n_a // FACE):
        own = jnp.broadcast_to(ids[band : band + 1].astype(jnp.float32), (8, blocks))
        cells = jnp.dot(own, spread, precision=HIGHEST)[:1]
        onehots.append((jnp.abs(cells - numbers.astype(jnp.float32)) < 0.5).astype(jnp.float32))

    def weigh(b, cols):
        for j in range(UNROLL):
            r = b * UNROLL + j
            own = eta[r + 1]
            near = shifted(0, b, j, COMPS, own, cols)
            below, above, west, east = (harmonic(own, other) for other in near)
            down = harmonic(own, eta[r]) if j == 0 else up
            up = harmonic(own, eta[r + 2])
            w_lat[0, r] = below
            w_lat[1, r] = above
            w_lon[0, r] = west
            w_lon[1, r] = east
            w_rad[r] = down
            w_rad[r + 1] = up
            d = 0.5 * own + (below + above) + (west + east) + (up + down)
            diag[r] = d
            gain[r] = RELAX / d

    def flux(t, b, j, c, cols):
        r = b * UNROLL + j
        tile = v[t][c, r + 1]
        below, above, west, east = shifted(t, b, j, c, tile, cols)
        total = (
            (w_lat[0, r] * below + w_lat[1, r] * above)
            + (w_lon[0, r] * west + w_lon[1, r] * east)
            + (w_rad[r] * v[t][c, r] + w_rad[r + 1] * v[t][c, r + 2])
        )
        return tile, f[c, r] + total

    def s1_copy(step):
        return pltpu.make_async_remote_copy(
            stage_out.at[0], lat_sums.at[me_lat], s1_send.at[step - 1], s1_recv.at[me_lat],
            device_id={"lat": lax.rem(me_lat + step, n_lat)}, device_id_type=MESH,
        )

    def s2_copy(step):
        return pltpu.make_async_remote_copy(
            stage_out.at[1], lon_sums.at[me_lon], s2_send.at[step - 1], s2_recv.at[me_lon],
            device_id={
                "lon": lax.rem(me_lon + step // n_rad, n_lon),
                "rad": lax.rem(me_rad + step % n_rad, n_rad),
            },
            device_id_type=MESH,
        )

    def received(buffer, sem, index):
        pltpu.make_async_remote_copy(
            stage_out.at[0], buffer.at[index], s1_send.at[0], sem.at[index],
            device_id={"lon": lon_up}, device_id_type=MESH,
        ).wait_recv()

    def torques():
        drag = [eta[n_r] * (last[c, n_r] - last[c, n_r - 1]) for c in range(COMPS)]
        twist = (
            (ry * drag[2] - rz * drag[1]) * cos_lat,
            (rz * drag[0] - rx * drag[2]) * cos_lat,
            (rx * drag[1] - ry * drag[0]) * cos_lat,
            cos_lat,
        )
        packed = jnp.zeros((1, LANES), jnp.float32)
        for band in range(n_a // FACE):
            cut = slice(band * FACE, (band + 1) * FACE)
            rows = jnp.concatenate(
                [jnp.sum(x[cut], axis=0, keepdims=True) for x in twist]
                + [jnp.zeros((4, n_o), jnp.float32)], 0,
            )
            sums = lax.dot_general(
                rows, onehots[band], (((1,), (1,)), ((), ())), precision=HIGHEST,
                preferred_element_type=jnp.float32,
            )
            packed = packed + jnp.concatenate([sums[i : i + 1] for i in range(COMPS + 1)], 1)
        stage_out[0] = packed
        lat_sums[me_lat] = packed
        for step in range(1, n_lat):
            s1_copy(step).start()

    for t in range(SWEEPS):
        for b in order:
            arrive(t, b)
            cols_in = (col_in[t, b, 0], col_in[t, b, 1])
            if t == 0:
                weigh(b, cols_in)
                if b == order[0]:
                    loads[2].wait()
            cols = no_cols
            for j in range(UNROLL):
                r = b * UNROLL + j
                for c in range(COMPS):
                    tile, total = flux(t, b, j, c, cols_in)
                    fresh = (1.0 - RELAX) * tile + gain[r] * total
                    v[t + 1][c, r + 1] = fresh
            for j in range(UNROLL):
                for c in range(COMPS):
                    cols = pack(t + 1, b, j, c, v[t + 1][c, b * UNROLL + j + 1], cols)
            put_cols(t + 1, b, cols)
            if t == SWEEPS - 1 and b == blocks_r - 1:
                pl.when(is_top)(torques)
            start(t + 1, b)

    @pl.when(is_top)
    def _():
        for step in range(1, n_lat):
            received(lat_sums, s1_recv, lax.rem(me_lat + step, n_lat))
        total = lat_sums[0]
        for i in range(1, n_lat):
            total = total + lat_sums[i]
        stage_out[1] = total
        lon_sums[me_lon] = total
        for step in range(1, n_lon * n_rad):
            s2_copy(step).start()

    for b in order:
        arrive(SWEEPS, b)
        cols_in = (col_in[SWEEPS, b, 0], col_in[SWEEPS, b, 1])
        for i in range(UNROLL // 2):
            for c in range(COMPS):
                two = jnp.zeros((n_a, n_o), jnp.float32)
                for j in (2 * i, 2 * i + 1):
                    tile, total = flux(SWEEPS, b, j, c, cols_in)
                    two = two + (total - diag[b * UNROLL + j] * tile)
                at = pl.ds((c * (n_r // 2) + b * (UNROLL // 2) + i) * n_a, n_a)
                for h in range(reps):
                    pairs[h, at] = two[:, h * LANES : (h + 1) * LANES]
    half = n_o // 2
    thin_r = lax.broadcasted_iota(jnp.int32, (LANES, half), 0)
    thin_c = lax.broadcasted_iota(jnp.int32, (LANES, half), 1)
    count = COMPS * (n_r // 2) * n_a // 2
    merged = jnp.zeros((count, half), jnp.float32)
    for h in range(reps):
        pick = jnp.where((thin_r + h * LANES) // 2 == thin_c, 0.125, 0.0).astype(jnp.bfloat16)
        both = pairs[h, pl.ds(0, count, stride=2)] + pairs[h, pl.ds(1, count, stride=2)]
        big = both.astype(jnp.bfloat16)
        small = (both - big.astype(jnp.float32)).astype(jnp.bfloat16)
        merged = merged + (
            jnp.dot(big, pick, preferred_element_type=jnp.float32)
            + jnp.dot(small, pick, preferred_element_type=jnp.float32)
        )
    mine = count // COMPS
    spot = pl.ds(pl.multiple_of(me_rad * mine, mine), mine)
    for c in range(COMPS):
        coarse[c, spot] = merged[c * mine : (c + 1) * mine]

    def g_copy(step):
        return pltpu.make_async_remote_copy(
            coarse.at[:, spot], coarse.at[:, spot], g_send.at[step - 1], g_recv.at[me_rad],
            device_id={"rad": lax.rem(me_rad + step, n_rad)}, device_id_type=MESH,
        )

    for step in range(1, n_rad):
        g_copy(step).start()

    for i in range(n_lon):
        @pl.when(jnp.logical_or(jnp.logical_not(is_top), me_lon != i))
        def _():
            received(lon_sums, s2_recv, i)
    total = lon_sums[0]
    for i in range(1, n_lon):
        total = total + lon_sums[i]
    area = total[:, COMPS * SLOT : (COMPS + 1) * SLOT]
    valid = lax.broadcasted_iota(jnp.int32, (1, SLOT), 1) < PLATES
    root = jnp.sqrt(jnp.where(valid, area, 1.0))
    turns = jnp.concatenate(
        [total[:, i * SLOT : (i + 1) * SLOT] / root for i in range(COMPS)]
        + [jnp.zeros((8 - COMPS, SLOT), jnp.float32)], 0,
    )
    for band in range(n_a // FACE):
        cut = slice(band * FACE, (band + 1) * FACE)
        cell = jnp.dot(turns, onehots[band], precision=HIGHEST, preferred_element_type=jnp.float32)
        ox, oy, oz = (cell[i : i + 1] for i in range(COMPS))
        plate[0, cut] = oy * rz[cut] - oz * ry[cut]
        plate[1, cut] = oz * rx[cut] - ox * rz[cut]
        plate[2, cut] = ox * ry[cut] - oy * rx[cut]

    for t in range(SWEEPS + 1):
        sent(t)

    @pl.when(is_top)
    def _():
        for step in range(1, n_lat):
            s1_copy(step).wait_send()
        for step in range(1, n_lon * n_rad):
            s2_copy(step).wait_send()

    for step in range(1, n_rad):
        source = lax.rem(me_rad + step, n_rad)
        region = coarse.at[:, pl.ds(pl.multiple_of(source * mine, mine), mine)]
        pltpu.make_async_remote_copy(
            region, region, g_send.at[0], g_recv.at[source],
            device_id={"rad": source}, device_id_type=MESH,
        ).wait_recv()
        g_copy(step).wait_send()


def write_out(last, coarse, plate, new_v_out, coarse_out, plate_out, sem):
    n_r = new_v_out.shape[1]
    copies = [
        pltpu.make_async_copy(last.at[:, pl.ds(1, n_r)], new_v_out, sem.at[0]),
        pltpu.make_async_copy(coarse, coarse_out, sem.at[1]),
        pltpu.make_async_copy(plate, plate_out, sem.at[2]),
    ]
    for copy in copies:
        copy.start()
    for copy in copies:
        copy.wait()


def on_device(sizes, velocity, forcing, viscosity, plate_ids):
    n_lat, n_lon, n_rad = sizes
    _, n_r, n_a, n_o = velocity.shape
    rounds = SWEEPS + 1
    chunks = n_r // UNROLL
    f32 = jnp.float32
    dma = pltpu.SemaphoreType.DMA
    in_any = pl.BlockSpec(memory_space=pl.ANY)
    in_vmem = pl.BlockSpec(memory_space=pltpu.VMEM)
    coarse_rows = n_rad * (n_r // 2) * (n_a // 2)
    held = pl.pallas_call(
        functools.partial(kernel, sizes),
        out_shape=(
            pltpu.VMEM((COMPS, n_r + 2, n_a, n_o), f32),
            pltpu.VMEM((COMPS, coarse_rows, n_o // 2), f32),
            pltpu.VMEM((COMPS, n_a, n_o), f32),
        ),
        in_specs=[pl.BlockSpec(memory_space=pltpu.HBM)] * 4,
        out_specs=(in_vmem,) * 3,
        scratch_shapes=[
            pltpu.VMEM((SWEEPS, COMPS, n_r + 2, n_a, n_o), f32),
            pltpu.VMEM(plate_ids.shape, jnp.int32),
            pltpu.VMEM((COMPS, n_r, n_a, n_o), f32),
            pltpu.VMEM((n_r + 2, n_a, n_o), f32),
            pltpu.VMEM((2, n_r, n_a, n_o), f32),
            pltpu.VMEM((2, n_r, n_a, n_o), f32),
            pltpu.VMEM((n_r + 1, n_a, n_o), f32),
            pltpu.VMEM((n_r, n_a, n_o), f32),
            pltpu.VMEM((n_r, n_a, n_o), f32),
            pltpu.VMEM((rounds, 2, (COMPS + 1) * n_r, 1, n_o), f32),
            pltpu.VMEM((rounds, 2, (COMPS + 1) * n_r, 1, n_o), f32),
            pltpu.VMEM((rounds, chunks, 2, n_a, LANES), f32),
            pltpu.VMEM((rounds, chunks, 2, n_a, LANES), f32),
            pltpu.VMEM((n_o // LANES, COMPS * (n_r // 2) * n_a, LANES), f32),
            pltpu.VMEM((n_lat, 1, LANES), f32),
            pltpu.VMEM((n_lon, 1, LANES), f32),
            pltpu.VMEM((2, 1, LANES), f32),
            dma((4,)),
            dma((rounds, chunks, 8)),
            dma((rounds, chunks, 8)),
            dma((n_lat,)),
            dma((n_lat,)),
            dma((n_lon * n_rad,)),
            dma((n_lon,)),
            dma((n_rad,)),
            dma((n_rad,)),
        ],
        compiler_params=pltpu.CompilerParams(
            collective_id=0, has_side_effects=True, vmem_limit_bytes=24 * 2**20
        ),
    )(*(
        pltpu.with_memory_space_constraint(x, pltpu.HBM)
        for x in (velocity, forcing, viscosity, plate_ids)
    ))
    new_v, coarse, plate = pl.pallas_call(
        write_out,
        out_shape=(
            jax.ShapeDtypeStruct(velocity.shape, f32),
            jax.ShapeDtypeStruct((COMPS, coarse_rows, n_o // 2), f32),
            jax.ShapeDtypeStruct((COMPS, n_a, n_o), f32),
        ),
        in_specs=[in_vmem] * 3,
        out_specs=(in_any,) * 3,
        scratch_shapes=[dma((3,))],
        compiler_params=pltpu.CompilerParams(vmem_limit_bytes=4 * 2**20),
    )(*(pltpu.with_memory_space_constraint(x, pltpu.VMEM) for x in held))
    coarse = coarse.reshape(COMPS, n_rad * (n_r // 2), n_a // 2, n_o // 2)
    return new_v, coarse, plate


def solution(mesh):
    sizes = tuple(mesh.shape[a] for a in ("lat", "lon", "rad"))
    field = P(None, "rad", "lat", "lon")
    return jax.shard_map(
        functools.partial(on_device, sizes),
        mesh=mesh,
        in_specs=(field, field, P("rad", "lat", "lon"), P("lat", "lon")),
        out_specs=(field, P(None, None, "lat", "lon"), P(None, "lat", "lon")),
        check_vma=False,
    )
```
